32 devices in a mesh: grp: 2 (over x), tm: 16 (over z, y, core).
Axes of the slice: x: 2, y: 2, z: 4, core: 2. Of those that a mesh axis runs over, the one named last changes fastest.
Arguments:
- queries: bfloat16 [24576, 128], P(('grp', 'tm')), parts along dimension 0, may hold values from -6 to 6
- key_codes: bfloat16 [24576, 128], P(('grp', 'tm')), parts along dimension 0, may hold values from -6 to 6
- value_codes: bfloat16 [24576, 128], P(('grp', 'tm')), parts along dimension 0, may hold values from -6 to 6
- key_scales: float32 [192], P(('grp', 'tm')), parts along dimension 0, may hold values from 0.6 to 1.6
- value_scales: float32 [192], P(('grp', 'tm')), parts along dimension 0, may hold values from 0.3 to 3
- scale_slot: int32 [32, 6], P(('grp', 'tm')), parts along dimension 0, may hold values from 0 to 5, each once within a row
- grad_out: bfloat16 [24576, 128], P(('grp', 'tm')), parts along dimension 0, may hold values from -384 to 384
Outputs:
- query_grad: bfloat16 [24576, 128], P(('grp', 'tm')), parts along dimension 0
- key_grad: bfloat16 [24576, 128], P(('grp', 'tm')), parts along dimension 0
- value_grad: bfloat16 [24576, 128], P(('grp', 'tm')), parts along dimension 0
The draws below stay inside these ranges and needn't reach their ends.
There are 2 independent parts, one for each index of `grp`. The reference program is written for one: setup_inputs(seed, part) draws one part's arguments, and reference() takes and returns one part's arrays. A program takes and returns all parts, laid end to end along the dimension named above; each array names one. Nothing has to cross between parts.
Inputs may be any that keep to these rules, and one draw needn't show every extreme that they name: Row s of scale_slot names every number 0 to 5 once.
All inputs are finite; a program needn't handle non-finite values.
Results may differ from the reference program's by a relative error of at most 0.0019.
The reference program's roundings to bfloat16 on the way count: a program that leaves them out, or rounds other values in their place, can miss the bound.
Values may be sent and summed in bfloat16 or wider, within the bound.
A program may use at most 64 MiB of HBM per device.

```python
import math
import jax
import jax.numpy as jnp
from jax import lax

HEAD_DIM = 128
TILE_TOKENS = 256
ROW_TILES = 4
QUANT_BLOCK = 128
FRAME_TILES = 4
TOK_DEV = 768
SLABS = 16
TOKENS = 12288
BLOCKS_DEV = 6
BLOCKS = 96


def draw_queries(key, part):
    own_key = jax.random.fold_in(key, 17)
    result = jax.random.truncated_normal(own_key, -6.0, 6.0, (TOKENS, HEAD_DIM), jnp.float32)
    return result.astype(jnp.bfloat16)


def draw_key_codes(key, part):
    own_key = jax.random.fold_in(key, 23)
    result = jax.random.truncated_normal(own_key, -6.0, 6.0, (TOKENS, HEAD_DIM), jnp.float32)
    return result.astype(jnp.bfloat16)


def levels(rng, shape, split, low, high):
    factor_of = 1.0
    for dim, parts in split:
        steps = jax.random.uniform(jax.random.fold_in(jax.random.fold_in(rng, 6), dim), (parts,), jnp.float32, low / len(split), high / len(split))
        factor_of = factor_of * jnp.repeat(jnp.exp(steps), shape[dim] // parts).reshape((-1,) + (1,) * (len(shape) - 1 - dim))
    return factor_of


def bell_draw(rng, dims, scale, limit, pieces=(), kind=jnp.bfloat16):
    loudness = levels(rng, dims, pieces, -0.22, 0.18) if pieces else 1.0
    values = jax.random.normal(rng, dims, jnp.float32) * scale * loudness
    return jnp.minimum(jnp.maximum(values, -limit), limit).astype(kind)


def setup_inputs(seed: int = 0, part: int = 0) -> dict:
    streams_of = jax.random.split(jax.random.key(seed), 8)
    own_keys = jax.random.split(jax.random.fold_in(streams_of[7], part), 8)
    queries = draw_queries(jax.random.fold_in(jax.random.fold_in(streams_of[7], part), 71), part)
    key_codes = draw_key_codes(jax.random.fold_in(jax.random.fold_in(streams_of[7], part), 71), part)
    value_codes = bell_draw(own_keys[2], (TOKENS, HEAD_DIM), 1.0, 6.0, ((0, 16),))
    key_scales = jnp.clip(jnp.exp(math.log(1.6) - 0.98082923 * jax.random.uniform(own_keys[3], (BLOCKS,), jnp.float32) ** levels(own_keys[3], (BLOCKS,), ((0, 16),), -0.2, 0.2)), 0.6, 1.6)
    value_scales = jnp.clip(jnp.exp(math.log(3.0) - 2.3025851 * jax.random.uniform(own_keys[4], (BLOCKS,), jnp.float32) ** levels(own_keys[4], (BLOCKS,), ((0, 16),), -0.2, 0.2)), 0.3, 3.0)
    scale_slot = jax.vmap(lambda own: jax.random.permutation(own, BLOCKS_DEV))(jax.random.split(own_keys[5], SLABS)).reshape((SLABS, BLOCKS_DEV)).astype(jnp.int32)
    grad_out = bell_draw(own_keys[6], (TOKENS, HEAD_DIM), 64.0, 384.0, ((0, 16),))
    return dict(queries=queries, key_codes=key_codes, value_codes=value_codes, key_scales=key_scales, value_scales=value_scales, scale_slot=scale_slot, grad_out=grad_out)


big_negative = -1.0e30
offsets_list = [(frame_step, row_step) for frame_step in (-1, 0, 1) for row_step in (-1, 0, 1)]


def dequantize(code_array, scales, scale_slot):
    slab_base = jnp.arange(SLABS, dtype=jnp.int32)[:, None] * BLOCKS_DEV
    scale_rows = (slab_base + scale_slot).reshape(-1)
    picked = scales[scale_rows]
    blocked = code_array.astype(jnp.float32).reshape(BLOCKS, QUANT_BLOCK, HEAD_DIM)
    return (blocked * picked[:, None, None]).astype(jnp.bfloat16).reshape(TOKENS, HEAD_DIM)


def reference(queries, key_codes, value_codes, key_scales, value_scales, scale_slot, grad_out):
    inverse = HEAD_DIM ** -0.5
    keys_all = dequantize(key_codes, key_scales, scale_slot)
    values_all = dequantize(value_codes, value_scales, scale_slot)

    def padded(array):
        tail_shape = array.shape[1:]
        shaped = array.reshape((FRAME_TILES, ROW_TILES, TOK_DEV) + tail_shape)
        widths = ((1, 1), (1, 1), (0, 0)) + tuple((0, 0) for extent in tail_shape)
        return jnp.pad(shaped, widths)

    zero_index = jnp.zeros((), jnp.int32)

    def take(array_pad, frame_idx, row_idx):
        starts = (frame_idx + 1, row_idx + 1) + tuple(zero_index for extent in array_pad.shape[2:])
        sizes_tuple = (1, 1) + array_pad.shape[2:]
        return lax.dynamic_slice(array_pad, starts, sizes_tuple)[0, 0]

    def inside(frame_idx, row_idx):
        return (frame_idx >= 0) & (frame_idx < FRAME_TILES) & (row_idx >= 0) & (row_idx < ROW_TILES)

    tile_of = jnp.arange(TOK_DEV, dtype=jnp.int32) // TILE_TOKENS
    near_cols = jnp.abs(tile_of[:, None] - tile_of[None, :]) <= 1
    query_pad = padded(queries)
    key_pad = padded(keys_all)
    value_pad = padded(values_all)
    grad_pad = padded(grad_out)

    def forward_slab(slab_id):
        frame_idx = slab_id // ROW_TILES
        row_idx = slab_id % ROW_TILES
        query_block = take(query_pad, frame_idx, row_idx)
        grad_block = take(grad_pad, frame_idx, row_idx)
        score_list, prob_grads, allowed_list, key_list = [], [], [], []
        for frame_step, row_step in offsets_list:
            other_frame = frame_idx + frame_step
            other_row = row_idx + row_step
            key_block = take(key_pad, other_frame, other_row)
            value_block = take(value_pad, other_frame, other_row)
            allowed = near_cols & inside(other_frame, other_row)
            scores = jnp.dot(query_block, key_block.T, preferred_element_type=jnp.float32) * inverse
            score_list.append(jnp.where(allowed, scores, big_negative))
            prob_grads.append(jnp.dot(grad_block, value_block.T, preferred_element_type=jnp.float32))
            allowed_list.append(allowed)
            key_list.append(key_block)
        scores = jnp.concatenate(score_list, axis=1)
        allowed_all = jnp.concatenate(allowed_list, axis=1)
        grad_prob = jnp.concatenate(prob_grads, axis=1)
        row_top = jnp.max(scores, axis=1, keepdims=True)
        summed = jnp.sum(jnp.where(allowed_all, jnp.exp(scores - row_top), 0.0), axis=1)
        log_total = row_top[:, 0] + jnp.log(summed)
        attn_prob = jnp.where(allowed_all, jnp.exp(scores - log_total[:, None]), 0.0)
        row_delta = jnp.sum(attn_prob * grad_prob, axis=1)
        dscore = (attn_prob * (grad_prob - row_delta[:, None])).astype(jnp.bfloat16)
        key_window = jnp.concatenate(key_list, axis=0)
        query_grad = (jnp.dot(dscore, key_window, preferred_element_type=jnp.float32) * inverse).astype(jnp.bfloat16)
        return query_grad, log_total, row_delta

    slab_ids = jnp.arange(SLABS, dtype=jnp.int32)
    query_grads, log_totals, row_deltas = lax.map(forward_slab, slab_ids)
    total_pad = padded(log_totals.reshape(TOKENS))
    delta_pad = padded(row_deltas.reshape(TOKENS))

    def backward_slab(slab_id):
        frame_idx = slab_id // ROW_TILES
        row_idx = slab_id % ROW_TILES
        key_block = take(key_pad, frame_idx, row_idx)
        value_block = take(value_pad, frame_idx, row_idx)
        key_sum = jnp.zeros((TOK_DEV, HEAD_DIM), jnp.float32)
        value_sum = jnp.zeros((TOK_DEV, HEAD_DIM), jnp.float32)
        for frame_step, row_step in offsets_list:
            other_frame = frame_idx + frame_step
            other_row = row_idx + row_step
            query_block = take(query_pad, other_frame, other_row)
            grad_block = take(grad_pad, other_frame, other_row)
            total_block = take(total_pad, other_frame, other_row)
            delta_block = take(delta_pad, other_frame, other_row)
            allowed = near_cols & inside(other_frame, other_row)
            scores = jnp.dot(query_block, key_block.T, preferred_element_type=jnp.float32) * inverse
            attn_prob = jnp.where(allowed, jnp.exp(scores - total_block[:, None]), 0.0)
            grad_prob = jnp.dot(grad_block, value_block.T, preferred_element_type=jnp.float32)
            dscore = (attn_prob * (grad_prob - delta_block[:, None])).astype(jnp.bfloat16)
            key_part = jnp.dot(dscore.T, query_block, preferred_element_type=jnp.float32) * inverse
            value_part = jnp.dot(attn_prob.astype(jnp.bfloat16).T, grad_block, preferred_element_type=jnp.float32)
            key_sum = key_sum + lax.optimization_barrier(key_part.astype(jnp.bfloat16)).astype(jnp.float32)
            value_sum = value_sum + lax.optimization_barrier(value_part.astype(jnp.bfloat16)).astype(jnp.float32)
        return key_sum.astype(jnp.bfloat16), value_sum.astype(jnp.bfloat16)

    key_grads, value_grads = lax.map(backward_slab, slab_ids)
    return (query_grads.reshape(TOKENS, HEAD_DIM), key_grads.reshape(TOKENS, HEAD_DIM), value_grads.reshape(TOKENS, HEAD_DIM))
```

```python
import functools
import math

import jax
import jax.numpy as jnp
from jax import lax
from jax.experimental import pallas as pl
from jax.experimental.pallas import tpu as pltpu
from jax.sharding import PartitionSpec as P

HEAD_DIM = 128
TILE_TOKENS = 256
ROW_TILES = 4
CHIP_DEVICES = 2
KEY, VALUE, QUERY, GRAD = range(4)

MESH = pl.DeviceIdType.MESH
OFFSETS = ((0, 0), (0, -1), (0, 1), (-1, 0), (1, 0), (-1, -1), (-1, 1), (1, -1), (1, 1))
POSITION = {offset: position for position, offset in enumerate(OFFSETS)}
TURNS = ((0, 2, 1, 3, 4, 6, 8, 5, 7), (0, 1, 2, 3, 4, 5, 7, 6, 8))
STEPS = (
    (0, 0), (1, 0), (0, 1), (1, 1), (0, 2), (1, 2), (0, 3), (0, 4), (0, 5), (0, 6),
    (1, 3), (1, 4), (1, 5), (1, 6), (0, 7), (0, 8), (1, 7), (1, 8),
)
INVERSE = HEAD_DIM ** (-0.5)
LOG2_SCALE = INVERSE * math.log2(math.e)


def dot_nt(left, right):
    return lax.dot_general(left, right, (((1,), (1,)), ((), ())), preferred_element_type=jnp.float32)


def dot_tn(left, right):
    return lax.dot_general(left, right, (((0,), (0,)), ((), ())), preferred_element_type=jnp.float32)


def near_range(tile, tiles):
    return max(0, tile - 1) * TILE_TOKENS, min(tiles, tile + 2) * TILE_TOKENS


def chosen(position, part):
    value = jnp.int32(0)
    for index, offset in enumerate(OFFSETS):
        if offset[part]:
            value = jnp.where(position == index, jnp.int32(offset[part]), value)
    return value


def kernel(frames, rows, q_in, k_in, v_in, g_in, k_scales, v_scales, slot_in, dq_out, dk_out, dv_out,
           data, codes, stats, e_all, dp_all, m_rec, w_rec, m_run, l_run, w_run, dq_acc, dk_acc, dv_acc, dk_part, dv_part,
           in_sem, send_sem, recv_sem, st_send, st_recv):
    me = lax.axis_index("tm")
    frame, row = me // rows, me % rows
    tokens = q_in.shape[0]
    tiles = tokens // TILE_TOKENS

    def inside(frame_step, row_step):
        f, r = frame + frame_step, row + row_step
        return (f >= 0) & (f < frames) & (r >= 0) & (r < rows)

    def at_turn(turn):
        position = turn
        odd = row % CHIP_DEVICES == CHIP_DEVICES - 1
        for index in range(len(OFFSETS)):
            if TURNS[0][index] != index or TURNS[1][index] != index:
                slot = jnp.where(odd, jnp.int32(TURNS[1][index]), jnp.int32(TURNS[0][index]))
                position = jnp.where(turn == index, slot, position)
        return position

    def crossing(row_step):
        return jnp.minimum(row, row + row_step) % CHIP_DEVICES == CHIP_DEVICES - 1

    def neighbour(frame_step, row_step):
        return {"tm": me + frame_step * rows + row_step}

    loads = [
        pltpu.make_async_copy(source, target, in_sem.at[index])
        for index, (source, target) in enumerate(
            ((v_in, codes.at[0]), (k_in, codes.at[1]), (q_in, data.at[0, QUERY]), (g_in, data.at[0, GRAD]))
        )
    ]
    for load in loads:
        load.start()

    barrier = pltpu.get_barrier_semaphore()
    count = jnp.int32(0)
    for offset in OFFSETS[1:]:
        ok = inside(*offset)
        count = count + ok.astype(jnp.int32)

        @pl.when(ok)
        def _():
            pl.semaphore_signal(barrier, inc=1, device_id=neighbour(*offset), device_id_type=MESH)

    blocks = k_scales.shape[0]
    block = tokens // blocks
    for index, (part, scales) in enumerate(((VALUE, v_scales), (KEY, k_scales))):
        loads[index].wait()
        for place in range(blocks):
            span = pl.ds(place * block, block)
            scale = scales[slot_in[0, place]]
            data[0, part, span, :] = (codes[index, span, :].astype(jnp.float32) * scale).astype(jnp.bfloat16)
    for load in loads[2:]:
        load.wait()
    pl.semaphore_wait(barrier, count)

    def send(part, index, source, step):
        held = OFFSETS[source]
        target = POSITION[(held[0] - step[0], held[1] - step[1])]
        return pltpu.make_async_remote_copy(
            src_ref=data.at[source, part],
            dst_ref=data.at[target, part],
            send_sem=send_sem.at[part, index],
            recv_sem=recv_sem.at[part, target],
            device_id=neighbour(*step),
            device_id_type=MESH,
        )

    own_frame = ((0, 0, (-1, 0)), (1, 0, (1, 0)))
    own_row = ((2, 0, (0, -1)), (3, 0, (0, 1)))
    relay_row = ((4, 3, (0, -1)), (5, 3, (0, 1)), (6, 4, (0, -1)), (7, 4, (0, 1)))
    relay_frame = ((8, 1, (-1, 0)), (9, 1, (1, 0)), (10, 2, (-1, 0)), (11, 2, (1, 0)))

    def each(part, plans, action):
        for index, source, step in plans:
            held = OFFSETS[source]
            ok = inside(*step) & inside(*held)
            if source in (1, 2):
                if part in (KEY, QUERY):
                    continue
                ok = ok & crossing(held[1])
            elif source in (3, 4) and part in (VALUE, GRAD):
                ok = ok & jnp.logical_not(crossing(step[1]))

            @pl.when(ok)
            def _():
                action(send(part, index, source, step))

    def of(plans, source):
        return [plan for plan in plans if plan[1] == source]

    def start(copy):
        copy.start()

    each(VALUE, own_row, start)
    each(KEY, own_frame, start)
    each(KEY, own_row, start)
    each(VALUE, own_frame, start)
    each(GRAD, own_row, start)

    def arrived(part, position):
        step = (chosen(position, 0), chosen(position, 1))
        pltpu.make_async_remote_copy(
            src_ref=data.at[position, part],
            dst_ref=data.at[position, part],
            send_sem=send_sem.at[part, 0],
            recv_sem=recv_sem.at[part, position],
            device_id=neighbour(*step),
            device_id_type=MESH,
        ).wait_recv()

    def stats_arrived(position):
        step = (chosen(position, 0), chosen(position, 1))
        pltpu.make_async_remote_copy(
            src_ref=stats.at[position],
            dst_ref=stats.at[position],
            send_sem=st_send.at[0],
            recv_sem=st_recv.at[position],
            device_id=neighbour(*step),
            device_id_type=MESH,
        ).wait_recv()

    def forward(part, source, plans):
        @pl.when(inside(*OFFSETS[source]))
        def _():
            arrived(part, jnp.int32(source))
            each(part, of(plans, source), start)

    m_run[...] = jnp.full_like(m_run, -1e30)
    l_run[...] = jnp.zeros_like(l_run)
    w_run[...] = jnp.zeros_like(w_run)
    dq_acc[...] = jnp.zeros_like(dq_acc)
    dk_acc[...] = jnp.zeros_like(dk_acc)
    dv_acc[...] = jnp.zeros_like(dv_acc)

    starts, total = [], 0
    for tile in range(tiles):
        first, last = near_range(tile, tiles)
        starts.append(total)
        total += last - first

    def score_step(position):
        for tile in range(tiles):
            first, last = near_range(tile, tiles)
            own = pl.ds(tile * TILE_TOKENS, TILE_TOKENS)
            place = pl.ds(starts[tile], last - first)
            scores = dot_nt(data[position, KEY, first:last, :], data[0, QUERY, own, :]) * LOG2_SCALE
            old = m_run[:, own]
            new = jnp.maximum(old, jnp.max(scores, axis=0, keepdims=True))
            e = jnp.exp2(scores - new)
            m_run[:, own] = new
            m_rec[position, :, own] = new
            l_run[:, own] = l_run[:, own] * jnp.exp2(old - new) + jnp.sum(e, axis=0, keepdims=True)
            e_all[position, place, :] = e

    def value_step(position):
        for tile in range(tiles):
            first, last = near_range(tile, tiles)
            own = pl.ds(tile * TILE_TOKENS, TILE_TOKENS)
            place = pl.ds(starts[tile], last - first)
            grad_prob = dot_nt(data[position, VALUE, first:last, :], data[0, GRAD, own, :])
            w_rec[position, :, own] = jnp.sum(e_all[position, place, :] * grad_prob, axis=0, keepdims=True)
            dp_all[position, place, :] = grad_prob

    def stat_pass(step, carry):
        turn, is_value = jnp.int32(0), jnp.int32(0)
        for index, (with_value, which) in enumerate(STEPS):
            turn = jnp.where(step == index, jnp.int32(which), turn)
            is_value = jnp.where(step == index, jnp.int32(with_value), is_value)
        position = at_turn(turn)
        valid = inside(chosen(position, 0), chosen(position, 1))

        for source in (1, 2):
            @pl.when((position == source) & (is_value == 1))
            def _():
                forward(VALUE, source, relay_frame)

        @pl.when(step == STEPS.index((0, 3)))
        def _():
            for part in (QUERY, GRAD):
                each(part, own_frame, start)
            for source in (3, 4):
                forward(KEY, source, relay_row)
            each(QUERY, own_row, start)

        @pl.when(step == STEPS.index((1, 3)))
        def _():
            for source in (3, 4):
                forward(VALUE, source, relay_row)

        @pl.when(step == STEPS.index((0, 7)))
        def _():
            for source in (1, 2):
                forward(GRAD, source, relay_frame)

        @pl.when(valid & (is_value == 0))
        def _():
            @pl.when((position > 0) & (position != 3) & (position != 4))
            def _():
                arrived(KEY, position)

            score_step(position)

        @pl.when(valid & (is_value == 1))
        def _():
            @pl.when(position > 4)
            def _():
                arrived(VALUE, position)

            value_step(position)

        return carry

    lax.fori_loop(0, len(STEPS), stat_pass, 0)

    def weigh(position, carry):
        @pl.when(inside(chosen(position, 0), chosen(position, 1)))
        def _():
            w_run[...] += w_rec[position] * jnp.exp2(m_rec[position] - m_run[...])

        return carry

    lax.fori_loop(0, len(OFFSETS), weigh, 0)
    stats[0, 0:1, :] = m_run[...] + jnp.log2(l_run[...])
    stats[0, 1:2, :] = w_run[...] / l_run[...]

    def stats_send(index):
        offset = OFFSETS[index]
        back = POSITION[(-offset[0], -offset[1])]
        return pltpu.make_async_remote_copy(
            src_ref=stats.at[0],
            dst_ref=stats.at[back],
            send_sem=st_send.at[index],
            recv_sem=st_recv.at[back],
            device_id=neighbour(*offset),
            device_id_type=MESH,
        )

    def query_pass(position, carry):
        @pl.when(position == 1)
        def _():
            for index in range(1, len(OFFSETS)):
                @pl.when(inside(*OFFSETS[index]))
                def _():
                    stats_send(index).start()

        @pl.when(inside(chosen(position, 0), chosen(position, 1)))
        def _():
            for tile in range(tiles):
                first, last = near_range(tile, tiles)
                own = pl.ds(tile * TILE_TOKENS, TILE_TOKENS)
                place = pl.ds(starts[tile], last - first)
                factor = jnp.exp2(m_rec[position, :, own] - stats[0, 0:1, own])
                prob = e_all[position, place, :] * factor
                dscore = (prob * (dp_all[position, place, :] - stats[0, 1:2, own])).astype(jnp.bfloat16)
                dq_acc[:, own] += dot_tn(data[position, KEY, first:last, :], dscore)

        return carry

    lax.fori_loop(0, len(OFFSETS), query_pass, 0)
    dq_out[...] = (dq_acc[...].T * INVERSE).astype(dq_out.dtype)

    def key_parts(position, known):
        done = 0
        for tile in range(tiles):
            first, last = near_range(tile, tiles)
            own = pl.ds(tile * TILE_TOKENS, TILE_TOKENS)
            query = data[position, QUERY, own, :]
            grad = data[position, GRAD, own, :]
            if known:
                place = pl.ds(starts[tile], last - first)
                prob = e_all[0, place, :] * jnp.exp2(m_rec[0, :, own] - stats[0, 0:1, own])
                grad_prob = dp_all[0, place, :]
            else:
                scores = dot_nt(data[0, KEY, first:last, :], query) * LOG2_SCALE
                prob = jnp.exp2(scores - stats[position, 0:1, own])
                grad_prob = dot_nt(data[0, VALUE, first:last, :], grad)
            dscore = (prob * (grad_prob - stats[position, 1:2, own])).astype(jnp.bfloat16)
            key_part = jnp.dot(dscore, query, preferred_element_type=jnp.float32)
            value_part = jnp.dot(prob.astype(jnp.bfloat16), grad, preferred_element_type=jnp.float32)
            if first < done:
                dk_part[first:done, :] += key_part[:done - first]
                dv_part[first:done, :] += value_part[:done - first]
            if done < last:
                dk_part[done:last, :] = key_part[done - first:]
                dv_part[done:last, :] = value_part[done - first:]
            done = last

    for source in (3, 4):
        forward(QUERY, source, relay_row)

    def key_pass(turn, carry):
        position = at_turn(turn)

        @pl.when(turn == 3)
        def _():
            for source in (3, 4):
                forward(GRAD, source, relay_row)

        @pl.when(inside(chosen(position, 0), chosen(position, 1)))
        def _():
            @pl.when(position > 0)
            def _():
                stats_arrived(position)

            @pl.when((position > 0) & (position != 3) & (position != 4))
            def _():
                arrived(QUERY, position)

            @pl.when(position > 4)
            def _():
                arrived(GRAD, position)

            @pl.when(position == 0)
            def _():
                key_parts(position, True)

            @pl.when(position > 0)
            def _():
                key_parts(position, False)

            key_part = (dk_part[...] * INVERSE).astype(jnp.bfloat16)
            dk_acc[...] += key_part.astype(jnp.float32)
            dv_acc[...] += dv_part[...].astype(jnp.bfloat16).astype(jnp.float32)

        return carry

    lax.fori_loop(0, len(OFFSETS), key_pass, 0)
    dk_out[...] = dk_acc[...].astype(dk_out.dtype)
    dv_out[...] = dv_acc[...].astype(dv_out.dtype)

    def sent(copy):
        copy.wait_send()

    for part in (KEY, VALUE, QUERY, GRAD):
        each(part, own_frame + own_row + relay_row + relay_frame, sent)
    for index in range(1, len(OFFSETS)):
        @pl.when(inside(*OFFSETS[index]))
        def _():
            stats_send(index).wait_send()


def put_out(dq_in, dk_in, dv_in, dq_out, dk_out, dv_out, out_sem):
    pairs = ((dq_in, dq_out), (dk_in, dk_out), (dv_in, dv_out))
    stores = [pltpu.make_async_copy(pair[0], pair[1], out_sem.at[i]) for i, pair in enumerate(pairs)]
    for store in stores:
        store.start()
    for store in stores:
        store.wait()


def per_device(queries, key_codes, value_codes, key_scales, value_scales, scale_slot, grad_out):
    rows = ROW_TILES
    frames = lax.axis_size("tm") // rows
    tokens, head_dim = queries.shape
    tiles = tokens // TILE_TOKENS
    near = sum(near_range(tile, tiles)[1] - near_range(tile, tiles)[0] for tile in range(tiles))
    slots = len(OFFSETS)
    shape = jax.ShapeDtypeStruct((tokens, head_dim), jnp.bfloat16)
    grads = pl.pallas_call(
        functools.partial(kernel, frames, rows),
        out_shape=(pltpu.VMEM((tokens, head_dim), jnp.bfloat16),) * 3,
        in_specs=[pl.BlockSpec(memory_space=pltpu.HBM)] * 4 + [pl.BlockSpec(memory_space=pltpu.SMEM)] * 3,
        out_specs=[pl.BlockSpec(memory_space=pltpu.VMEM)] * 3,
        scratch_shapes=[
            pltpu.VMEM((slots, 4, tokens, head_dim), jnp.bfloat16),
            pltpu.VMEM((2, tokens, head_dim), jnp.bfloat16),
            pltpu.VMEM((slots, 2, tokens), jnp.float32),
            pltpu.VMEM((slots, near, TILE_TOKENS), jnp.float32),
            pltpu.VMEM((slots, near, TILE_TOKENS), jnp.float32),
            pltpu.VMEM((slots, 1, tokens), jnp.float32),
            pltpu.VMEM((slots, 1, tokens), jnp.float32),
            pltpu.VMEM((1, tokens), jnp.float32),
            pltpu.VMEM((1, tokens), jnp.float32),
            pltpu.VMEM((1, tokens), jnp.float32),
            pltpu.VMEM((head_dim, tokens), jnp.float32),
            pltpu.VMEM((tokens, head_dim), jnp.float32),
            pltpu.VMEM((tokens, head_dim), jnp.float32),
            pltpu.VMEM((tokens, head_dim), jnp.float32),
            pltpu.VMEM((tokens, head_dim), jnp.float32),
            pltpu.SemaphoreType.DMA((4,)),
            pltpu.SemaphoreType.DMA((4, 12)),
            pltpu.SemaphoreType.DMA((4, slots)),
            pltpu.SemaphoreType.DMA((slots,)),
            pltpu.SemaphoreType.DMA((slots,)),
        ],
        compiler_params=pltpu.CompilerParams(
            collective_id=0, has_side_effects=True, vmem_limit_bytes=60 * 1024 * 1024
        ),
    )(queries, key_codes, value_codes, grad_out, key_scales, value_scales, scale_slot)
    return tuple(pl.pallas_call(
        put_out,
        out_shape=(shape, shape, shape),
        in_specs=[pl.BlockSpec(memory_space=pltpu.VMEM)] * 3,
        out_specs=[pl.BlockSpec(memory_space=pl.ANY)] * 3,
        scratch_shapes=[pltpu.SemaphoreType.DMA((3,))],
        compiler_params=pltpu.CompilerParams(vmem_limit_bytes=2 * 1024 * 1024),
    )(*grads))


def solution(mesh):
    in_specs = (
        P(("grp", "tm"), None),
        P(("grp", "tm"), None),
        P(("grp", "tm"), None),
        P(("grp", "tm")),
        P(("grp", "tm")),
        P(("grp", "tm"), None),
        P(("grp", "tm"), None),
    )
    out_specs = (P(("grp", "tm"), None), P(("grp", "tm"), None), P(("grp", "tm"), None))
    return jax.shard_map(
        per_device, mesh=mesh, in_specs=in_specs, out_specs=out_specs, check_vma=False
    )
```

```python
import functools
import math

import jax
import jax.numpy as jnp
from jax import lax
from jax.experimental import pallas as pl
from jax.experimental.pallas import tpu as pltpu
from jax.sharding import PartitionSpec as P

HEAD_DIM = 128
TILE_TOKENS = 256
ROW_TILES = 4
CHIP_DEVICES = 2
KEY, VALUE, QUERY, GRAD = range(4)

MESH = pl.DeviceIdType.MESH
INVERSE = HEAD_DIM ** (-0.5)
LOG2_SCALE = INVERSE * math.log2(math.e)

OWN, C, X, AM, AZ, BM, BZ, MX, ZX = range(9)
SLOTS = 9
NAMES = ("", "C", "X", "AM", "AZ", "BM", "BZ", "MX", "ZX")


def dot_nt(left, right):
    return lax.dot_general(left, right, (((1,), (1,)), ((), ())), preferred_element_type=jnp.float32)


def near_range(tile, tiles):
    return max(0, tile - 1) * TILE_TOKENS, min(tiles, tile + 2) * TILE_TOKENS


def kernel(frames, rows, q_in, k_in, v_in, g_in, k_scales, v_scales, slot_in, dq_out, dk_out, dv_out,
           data, codes, stats, e_all, dp_all, ps, ds, m_rec, w_rec, l_rec, dq_acc, dk_acc, dv_acc,
           part_out, part_in, in_sem, send_sem, recv_sem, st_send, st_recv, pt_send, pt_recv):
    me = lax.axis_index("tm")
    frame, row = me // rows, me % rows
    tokens = q_in.shape[0]
    tiles = tokens // TILE_TOKENS
    turn = 1 - 2 * (row % CHIP_DEVICES)

    inner = (row - turn >= 0) & (row - turn < rows)
    has = {"C": None, "A": None, "B": None, "X": inner, "M": frame > 0, "Z": frame < frames - 1}
    outer = jnp.logical_not(inner)
    shift = {
        "C": turn, "X": -turn, "M": -rows, "Z": rows,
        "A": jnp.where(inner, 0, turn), "B": jnp.where(inner, turn, 0),
    }
    names = NAMES

    def valid(text):
        ok = None
        for name in text:
            if has[name] is not None:
                ok = has[name] if ok is None else ok & has[name]
        return ok

    def device(text):
        return {"tm": me + sum(shift[name] for name in text)}

    def lands(source, way):
        if source == OWN and way in "MZ":
            return jnp.where(inner, AZ, BZ) if way == "M" else jnp.where(inner, AM, BM)
        fixed = {
            (OWN, "C"): C, (OWN, "X"): X, (AM, "X"): MX, (AZ, "X"): ZX, (X, "Z"): MX, (X, "M"): ZX,
        }
        return source if way == "C" and source != OWN else fixed[source, way]

    def guard(ok, action):
        if ok is None:
            action()
        else:
            pl.when(ok)(action)

    def masked(slot, value, other):
        ok = valid(names[slot])
        return value if ok is None else jnp.where(ok, value, other)

    def across(slot, value):
        return masked(slot, value, 0.0) if slot in (X, MX, ZX) else value

    def inner_rows(action):
        pl.when(inner)(action)

    loads = [
        pltpu.make_async_copy(source, target, in_sem.at[index])
        for index, (source, target) in enumerate(
            ((k_in, codes.at[0]), (v_in, codes.at[1]), (q_in, data.at[OWN, QUERY]), (g_in, data.at[OWN, GRAD]))
        )
    ]
    for load in loads:
        load.start()

    barrier = pltpu.get_barrier_semaphore()
    count = jnp.int32(1)
    for slot in range(1, SLOTS):
        ok = valid(names[slot])
        if ok is not None:
            count = count + ok.astype(jnp.int32)

        def greet():
            pl.semaphore_signal(barrier, inc=1, device_id=device(names[slot]), device_id_type=MESH)

        guard(ok, greet)

    for name, slots in (("M", (AM, BM)), ("Z", (AZ, BZ))):
        @pl.when(jnp.logical_not(has[name]))
        def _():
            for slot in slots:
                data[slot] = jnp.zeros_like(data[slot])
                stats[slot] = jnp.zeros_like(stats[slot])

    @pl.when(outer)
    def _():
        for slot in (X, MX, ZX):
            m_rec[slot] = jnp.full_like(m_rec[slot], -1e30)
            l_rec[slot] = jnp.zeros_like(l_rec[slot])
            w_rec[slot] = jnp.zeros_like(w_rec[slot])

    blocks = k_scales.shape[0]
    block = tokens // blocks

    def scale_codes(index, part, scales):
        loads[index].wait()
        for place in range(blocks):
            span = pl.ds(place * block, block)
            scale = scales[slot_in[0, place]]
            data[OWN, part, span, :] = (codes[index, span, :].astype(jnp.float32) * scale).astype(jnp.bfloat16)

    sent = []

    def send(part, source, way):
        target = lands(source, way)
        index = len([other for other in sent[:sent.index((part, source, way))] if other[0] == part])
        return pltpu.make_async_remote_copy(
            src_ref=data.at[source, part],
            dst_ref=data.at[target, part],
            send_sem=send_sem.at[part, index],
            recv_sem=recv_sem.at[part, target],
            device_id=device(way),
            device_id_type=MESH,
        )

    def condition(source, way):
        ok = valid(names[source] + way)
        if way == "C" and source in (AM, AZ):
            ok = inner if ok is None else ok & inner
        if way == "C" and source in (BM, BZ):
            ok = outer if ok is None else ok & outer
        return ok

    def push(part, source, way, only=None):
        if (part, source, way) not in sent:
            sent.append((part, source, way))
        ok = condition(source, way)
        if only is not None:
            ok = only if ok is None else ok & only
        guard(ok, lambda: send(part, source, way).start())

    def arrive(part, slot):
        copy = pltpu.make_async_remote_copy(
            src_ref=data.at[slot, part],
            dst_ref=data.at[slot, part],
            send_sem=send_sem.at[part, 0],
            recv_sem=recv_sem.at[part, slot],
            device_id=device(names[slot]),
            device_id_type=MESH,
        )
        guard(valid(names[slot]), copy.wait_recv)

    def relay(part, slot):
        arrive(part, slot)
        if slot in (AM, AZ, BM, BZ):
            push(part, slot, "C")
        if slot in (AM, AZ) and part in (KEY, QUERY):
            push(part, slot, "X")
        if slot == X and part in (VALUE, GRAD):
            push(part, slot, "M")
            push(part, slot, "Z")

    starts, total = [], 0
    for tile in range(tiles):
        first, last = near_range(tile, tiles)
        starts.append(total)
        total += last - first

    def columns(tile):
        first, last = near_range(tile, tiles)
        return first, last, pl.ds(tile * TILE_TOKENS, TILE_TOKENS), pl.ds(starts[tile], last - first)

    units = [
        (tile, start, pl.ds(starts[tile] + start - near_range(tile, tiles)[0], TILE_TOKENS))
        for tile in range(tiles)
        for start in range(*near_range(tile, tiles), TILE_TOKENS)
    ]

    def mix(*strands):
        marks = sorted(
            ((place + 0.5) / len(steps), which, place)
            for which, steps in enumerate(strands)
            for place in range(len(steps))
        )
        for _, which, place in marks:
            strands[which][place]()

    def op_s(slot):
        def unit(tile, start, place):
            own = pl.ds(tile * TILE_TOKENS, TILE_TOKENS)
            e_all[slot, place, :] = dot_nt(data[slot, KEY, start:start + TILE_TOKENS, :], data[OWN, QUERY, own, :])

        return [functools.partial(unit, *item) for item in units]

    def op_d(slot):
        def unit(tile, start, place):
            own = pl.ds(tile * TILE_TOKENS, TILE_TOKENS)
            dp_all[slot, place, :] = dot_nt(data[slot, VALUE, start:start + TILE_TOKENS, :], data[OWN, GRAD, own, :])

        return [functools.partial(unit, *item) for item in units]

    def op_e(slot):
        held = {}

        def top(tile, start, place):
            new = jnp.max(e_all[slot, place, :], axis=0, keepdims=True)
            held[tile] = new if tile not in held else jnp.maximum(held[tile], new)

        def power(tile, start, place, last):
            if ("top", tile) not in held:
                held["top", tile] = held[tile] * LOG2_SCALE
            e = jnp.exp2(e_all[slot, place, :] * LOG2_SCALE - held["top", tile])
            added = jnp.sum(e, axis=0, keepdims=True)
            held["sum", tile] = added if ("sum", tile) not in held else held["sum", tile] + added
            e_all[slot, place, :] = e
            if last:
                own = pl.ds(tile * TILE_TOKENS, TILE_TOKENS)
                m_rec[slot, :, own] = masked(slot, held["top", tile], -1e30)
                l_rec[slot, :, own] = masked(slot, held["sum", tile], 0.0)

        steps = []
        for tile in range(tiles):
            mine = [item for item in units if item[0] == tile]
            steps += [functools.partial(top, *item) for item in mine]
            steps += [functools.partial(power, *item, item is mine[-1]) for item in mine]
        return steps

    def op_w(slot):
        held = {}

        def unit(tile, start, place):
            added = jnp.sum(e_all[slot, place, :] * dp_all[slot, place, :], axis=0, keepdims=True)
            held[tile] = added if tile not in held else held[tile] + added
            if start + TILE_TOKENS == near_range(tile, tiles)[1]:
                w_rec[slot, :, pl.ds(tile * TILE_TOKENS, TILE_TOKENS)] = masked(slot, held[tile], 0.0)

        return [functools.partial(unit, *item) for item in units]

    def stats_send(slot):
        back = {C: C, X: X, MX: ZX, ZX: MX}.get(slot)
        if slot in (AM, BM):
            back = jnp.where(inner, AZ, BZ)
        if slot in (AZ, BZ):
            back = jnp.where(inner, AM, BM)
        return pltpu.make_async_remote_copy(
            src_ref=stats.at[OWN],
            dst_ref=stats.at[back],
            send_sem=st_send.at[slot],
            recv_sem=st_recv.at[back],
            device_id=device(names[slot]),
            device_id_type=MESH,
        )

    def op_total():
        top = m_rec[OWN]
        for slot in range(1, SLOTS):
            top = jnp.maximum(top, m_rec[slot])
        total = l_rec[OWN] * jnp.exp2(m_rec[OWN] - top)
        weighed = w_rec[OWN] * jnp.exp2(m_rec[OWN] - top)
        for slot in range(1, SLOTS):
            factor = jnp.exp2(m_rec[slot] - top)
            total += l_rec[slot] * factor
            weighed += w_rec[slot] * factor
        stats[OWN, 0:1, :] = top + jnp.log2(total)
        stats[OWN, 1:2, :] = weighed / total

    def op_q(slot, to):
        held = {}

        def unit(tile, start, place):
            own = pl.ds(tile * TILE_TOKENS, TILE_TOKENS)
            rows_of = pl.ds(start, TILE_TOKENS)
            if tile not in held:
                held[tile] = jnp.exp2(m_rec[slot, :, own] - stats[OWN, 0:1, own])
            if ("turned", start) not in held:
                held["turned", start] = data[slot, KEY, rows_of, :].T
            prob = e_all[slot, place, :] * held[tile]
            dscore = (prob * (dp_all[slot, place, :] - stats[OWN, 1:2, own])).astype(jnp.bfloat16)
            if to is not None:
                ps[to, rows_of, own] = prob.astype(jnp.bfloat16)
                ds[to, rows_of, own] = dscore
            added = jnp.dot(held["turned", start], dscore, preferred_element_type=jnp.float32)
            held["sum", tile] = added if ("sum", tile) not in held else held["sum", tile] + added
            if start + TILE_TOKENS == near_range(tile, tiles)[1]:
                if slot == OWN:
                    dq_acc[:, own] = held["sum", tile]
                else:
                    dq_acc[:, own] += across(slot, held["sum", tile])

        return [functools.partial(unit, *item) for item in units]

    def op_ks(slot):
        def unit(index, tile, start, place):
            own, near = pl.ds(tile * TILE_TOKENS, TILE_TOKENS), pl.ds(start, TILE_TOKENS)
            held = pl.ds(index * TILE_TOKENS, TILE_TOKENS)
            e_all[slot, held, :] = dot_nt(data[OWN, KEY, own, :], data[slot, QUERY, near, :])

        return [functools.partial(unit, index, *item) for index, item in enumerate(units)]

    def op_kd(slot):
        def unit(index, tile, start, place):
            own, near = pl.ds(tile * TILE_TOKENS, TILE_TOKENS), pl.ds(start, TILE_TOKENS)
            held = pl.ds(index * TILE_TOKENS, TILE_TOKENS)
            dp_all[slot, held, :] = dot_nt(data[OWN, VALUE, own, :], data[slot, GRAD, near, :])

        return [functools.partial(unit, index, *item) for index, item in enumerate(units)]

    def op_kv(slot, to):
        def unit(index, tile, start, place):
            own, near = pl.ds(tile * TILE_TOKENS, TILE_TOKENS), pl.ds(start, TILE_TOKENS)
            held = pl.ds(index * TILE_TOKENS, TILE_TOKENS)
            prob = jnp.exp2(e_all[slot, held, :] * LOG2_SCALE - stats[slot, 0:1, near])
            ps[to, own, near] = prob.astype(jnp.bfloat16)
            ds[to, own, near] = (prob * (dp_all[slot, held, :] - stats[slot, 1:2, near])).astype(jnp.bfloat16)

        return [functools.partial(unit, index, *item) for index, item in enumerate(units)]

    def op_m(slot, source):
        queries_of = OWN if slot == C else slot
        held = {}

        def unit(which, tile):
            part, right, acc = ((QUERY, ds, dk_acc), (GRAD, ps, dv_acc))[which]
            first, last, own, place = columns(tile)
            if which not in held:
                held[which] = data[queries_of, part].T
            summed = dot_nt(held[which][:, first:last], right[source, own, first:last])
            if part == QUERY:
                summed = summed * INVERSE
            rounded = summed.astype(jnp.bfloat16)
            if slot == C:
                part_out[which, :, own] = rounded
            elif slot == OWN:
                acc[:, own] = rounded.astype(jnp.float32)
            else:
                acc[:, own] += across(slot, rounded.astype(jnp.float32))

        return [functools.partial(unit, which, tile) for tile in range(tiles) for which in range(2)]

    def parts_send():
        return pltpu.make_async_remote_copy(
            src_ref=part_out, dst_ref=part_in, send_sem=pt_send, recv_sem=pt_recv,
            device_id=device("C"), device_id_type=MESH,
        )

    def stats_arrive(slot):
        copy = pltpu.make_async_remote_copy(
            src_ref=stats.at[slot], dst_ref=stats.at[slot], send_sem=st_send.at[slot], recv_sem=st_recv.at[slot],
            device_id=device(names[slot]), device_id_type=MESH,
        )
        guard(valid(names[slot]), copy.wait_recv)

    scale_codes(0, KEY, k_scales)
    pl.semaphore_wait(barrier, count)
    push(KEY, OWN, "M", inner)
    push(KEY, OWN, "Z", inner)
    scale_codes(1, VALUE, v_scales)
    push(VALUE, OWN, "C")
    push(KEY, OWN, "X")
    push(KEY, OWN, "C")
    push(VALUE, OWN, "X")
    arrive(VALUE, C)
    loads[3].wait()
    loads[2].wait()
    mix(op_d(C), op_s(OWN))

    mix(op_d(OWN))

    push(KEY, OWN, "M", outer)
    push(KEY, OWN, "Z", outer)
    push(VALUE, OWN, "M", outer)
    push(VALUE, OWN, "Z", outer)
    push(GRAD, OWN, "X")
    relay(KEY, AM)
    relay(KEY, AZ)
    relay(VALUE, X)
    push(VALUE, OWN, "M", inner)
    push(VALUE, OWN, "Z", inner)
    arrive(KEY, X)
    mix(op_s(X), op_s(AM))

    push(QUERY, OWN, "M", inner)
    push(QUERY, OWN, "Z", inner)
    relay(KEY, BZ)
    arrive(KEY, C)
    mix(op_s(BZ), op_s(C), op_s(AZ))

    relay(KEY, BM)
    mix(op_e(C), op_e(AZ), op_e(AM), op_s(BM))

    mix(op_e(OWN), op_e(BM))

    push(QUERY, OWN, "X")
    relay(VALUE, BM)
    push(GRAD, OWN, "M", inner)
    push(GRAD, OWN, "Z", inner)
    mix(op_e(X), op_w(OWN), op_d(BM), op_d(X))

    relay(VALUE, BZ)
    arrive(VALUE, MX)
    mix(op_e(BZ), op_w(BM), op_w(X), op_d(MX))

    arrive(KEY, ZX)
    arrive(VALUE, ZX)
    inner_rows(lambda: mix(op_s(ZX), op_d(ZX)))

    relay(GRAD, X)
    arrive(KEY, MX)
    mix(op_e(ZX), op_d(BZ), op_s(MX))

    relay(VALUE, AM)
    relay(VALUE, AZ)
    mix(op_e(MX), op_w(BZ), op_d(AM), op_d(AZ))

    mix(op_w(ZX), op_w(C), op_w(AZ), op_w(MX))

    mix(op_w(AM))

    push(GRAD, OWN, "M", outer)
    push(GRAD, OWN, "Z", outer)
    op_total()
    relay(QUERY, AM)
    relay(QUERY, AZ)
    mix(op_q(OWN, 0), op_q(AM, None))

    push(QUERY, OWN, "M", outer)
    push(QUERY, OWN, "Z", outer)
    mix(op_q(BM, None), op_q(AZ, None), op_m(OWN, 0))

    for slot in range(1, SLOTS):
        if slot != C:
            guard(valid(names[slot]), stats_send(slot).start)
    mix(op_q(BZ, None), op_q(C, 0), op_q(X, None), op_ks(AZ))

    relay(GRAD, AM)
    arrive(QUERY, X)
    mix(op_q(MX, None), op_kd(AM), op_ks(X), op_ks(AM))

    relay(GRAD, AZ)
    arrive(GRAD, MX)
    inner_rows(lambda: mix(op_q(ZX, None), op_kd(MX), op_kd(X)))

    arrive(QUERY, MX)
    stats_arrive(X)
    inner_rows(lambda: mix(op_kv(X, 1), op_ks(MX)))

    stats_arrive(AM)
    mix(op_kv(AM, 2), op_m(C, 0), op_kd(AZ))

    arrive(GRAD, ZX)
    stats_arrive(MX)
    arrive(QUERY, ZX)
    inner_rows(lambda: mix(op_kv(MX, 0), op_kd(ZX), op_ks(ZX), op_m(X, 1)))

    stats_arrive(ZX)
    inner_rows(lambda: mix(op_kv(ZX, 1), op_m(MX, 0)))

    relay(GRAD, BM)
    relay(GRAD, BZ)
    parts_send().start()
    stats_arrive(AZ)
    mix(op_kv(AZ, 0), op_m(AM, 2), op_kd(BZ), op_m(ZX, 1))

    relay(QUERY, BZ)
    relay(QUERY, BM)
    mix(op_ks(BZ), op_ks(BM), op_kd(BM))

    stats_arrive(BZ)
    stats_arrive(BM)
    mix(op_kv(BZ, 2), op_kv(BM, 1))

    parts_send().wait_recv()
    mix(op_m(BZ, 2), op_m(AZ, 0), op_m(BM, 1))

    dq_out[...] = (dq_acc[...] * INVERSE).astype(dq_out.dtype).T
    dk_out[...] = (dk_acc[...] + part_in[0].astype(jnp.float32)).astype(dk_out.dtype).T
    dv_out[...] = (dv_acc[...] + part_in[1].astype(jnp.float32)).astype(dv_out.dtype).T

    for key in sent:
        guard(condition(*key[1:]), send(*key).wait_send)
    for slot in range(1, SLOTS):
        if slot != C:
            guard(valid(names[slot]), stats_send(slot).wait_send)
    parts_send().wait_send()


def put_out(dq_in, dk_in, dv_in, dq_out, dk_out, dv_out, out_sem):
    pairs = ((dq_in, dq_out), (dk_in, dk_out), (dv_in, dv_out))
    stores = [pltpu.make_async_copy(pair[0], pair[1], out_sem.at[i]) for i, pair in enumerate(pairs)]
    for store in stores:
        store.start()
    for store in stores:
        store.wait()


def per_device(queries, key_codes, value_codes, key_scales, value_scales, scale_slot, grad_out):
    rows = ROW_TILES
    frames = lax.axis_size("tm") // rows
    tokens, head_dim = queries.shape
    tiles = tokens // TILE_TOKENS
    near = sum(near_range(tile, tiles)[1] - near_range(tile, tiles)[0] for tile in range(tiles))
    shape = jax.ShapeDtypeStruct((tokens, head_dim), jnp.bfloat16)
    grads = pl.pallas_call(
        functools.partial(kernel, frames, rows),
        out_shape=(pltpu.VMEM((tokens, head_dim), jnp.bfloat16),) * 3,
        in_specs=[pl.BlockSpec(memory_space=pltpu.HBM)] * 4 + [pl.BlockSpec(memory_space=pltpu.SMEM)] * 3,
        out_specs=[pl.BlockSpec(memory_space=pltpu.VMEM)] * 3,
        scratch_shapes=[
            pltpu.VMEM((SLOTS, 4, tokens, head_dim), jnp.bfloat16),
            pltpu.VMEM((2, tokens, head_dim), jnp.bfloat16),
            pltpu.VMEM((SLOTS, 2, tokens), jnp.float32),
            pltpu.VMEM((SLOTS, near, TILE_TOKENS), jnp.float32),
            pltpu.VMEM((SLOTS, near, TILE_TOKENS), jnp.float32),
            pltpu.VMEM((3, tokens, tokens), jnp.bfloat16),
            pltpu.VMEM((3, tokens, tokens), jnp.bfloat16),
            pltpu.VMEM((SLOTS, 1, tokens), jnp.float32),
            pltpu.VMEM((SLOTS, 1, tokens), jnp.float32),
            pltpu.VMEM((SLOTS, 1, tokens), jnp.float32),
            pltpu.VMEM((head_dim, tokens), jnp.float32),
            pltpu.VMEM((head_dim, tokens), jnp.float32),
            pltpu.VMEM((head_dim, tokens), jnp.float32),
            pltpu.VMEM((2, head_dim, tokens), jnp.bfloat16),
            pltpu.VMEM((2, head_dim, tokens), jnp.bfloat16),
            pltpu.SemaphoreType.DMA((4,)),
            pltpu.SemaphoreType.DMA((4, 10)),
            pltpu.SemaphoreType.DMA((4, SLOTS)),
            pltpu.SemaphoreType.DMA((SLOTS,)),
            pltpu.SemaphoreType.DMA((SLOTS,)),
            pltpu.SemaphoreType.DMA,
            pltpu.SemaphoreType.DMA,
        ],
        compiler_params=pltpu.CompilerParams(
            collective_id=0, has_side_effects=True, vmem_limit_bytes=60 * 1024 * 1024
        ),
    )(queries, key_codes, value_codes, grad_out, key_scales, value_scales, scale_slot)
    return tuple(pl.pallas_call(
        put_out,
        out_shape=(shape, shape, shape),
        in_specs=[pl.BlockSpec(memory_space=pltpu.VMEM)] * 3,
        out_specs=[pl.BlockSpec(memory_space=pl.ANY)] * 3,
        scratch_shapes=[pltpu.SemaphoreType.DMA((3,))],
        compiler_params=pltpu.CompilerParams(vmem_limit_bytes=2 * 1024 * 1024),
    )(*grads))


def solution(mesh):
    in_specs = (
        P(("grp", "tm"), None),
        P(("grp", "tm"), None),
        P(("grp", "tm"), None),
        P(("grp", "tm")),
        P(("grp", "tm")),
        P(("grp", "tm"), None),
        P(("grp", "tm"), None),
    )
    out_specs = (P(("grp", "tm"), None), P(("grp", "tm"), None), P(("grp", "tm"), None))
    return jax.shard_map(
        per_device, mesh=mesh, in_specs=in_specs, out_specs=out_specs, check_vma=False
    )
```

```python
import functools
import math

import jax
import jax.numpy as jnp
from jax import lax
from jax.experimental import pallas as pl
from jax.experimental.pallas import tpu as pltpu
from jax.sharding import PartitionSpec as P

HEAD_DIM = 128
TILE_TOKENS = 256
ROW_TILES = 4
CHIP_DEVICES = 2
KEY, VALUE, QUERY, GRAD = range(4)

MESH = pl.DeviceIdType.MESH
INVERSE = HEAD_DIM ** (-0.5)
LOG2_SCALE = INVERSE * math.log2(math.e)

OWN, C, X, AM, AZ, BM, BZ, MX, ZX = range(9)
SLOTS = 9
NAMES = ("", "C", "X", "AM", "AZ", "BM", "BZ", "MX", "ZX")


def dot_nt(left, right):
    return lax.dot_general(left, right, (((1,), (1,)), ((), ())), preferred_element_type=jnp.float32)


def near_range(tile, tiles):
    return max(0, tile - 1) * TILE_TOKENS, min(tiles, tile + 2) * TILE_TOKENS


def kernel(frames, rows, q_in, k_in, v_in, g_in, k_scales, v_scales, slot_in, dq_out, dk_out, dv_out,
           data, codes, stats, e_all, dp_all, ps, ds, m_rec, w_rec, l_rec, dq_acc, dk_acc, dv_acc,
           part_out, part_in, in_sem, send_sem, recv_sem, st_send, st_recv, pt_send, pt_recv):
    me = lax.axis_index("tm")
    frame, row = me // rows, me % rows
    tokens = q_in.shape[0]
    tiles = tokens // TILE_TOKENS
    turn = 1 - 2 * (row % CHIP_DEVICES)

    inner = (row - turn >= 0) & (row - turn < rows)
    has = {"C": None, "A": None, "B": None, "X": inner, "M": frame > 0, "Z": frame < frames - 1}
    outer = jnp.logical_not(inner)
    shift = {
        "C": turn, "X": -turn, "M": -rows, "Z": rows,
        "A": jnp.where(inner, 0, turn), "B": jnp.where(inner, turn, 0),
    }
    names = NAMES

    def valid(text):
        ok = None
        for name in text:
            if has[name] is not None:
                ok = has[name] if ok is None else ok & has[name]
        return ok

    def device(text):
        return {"tm": me + sum(shift[name] for name in text)}

    def lands(source, way):
        if source == OWN and way in "MZ":
            return jnp.where(inner, AZ, BZ) if way == "M" else jnp.where(inner, AM, BM)
        fixed = {
            (OWN, "C"): C, (OWN, "X"): X, (AM, "X"): MX, (AZ, "X"): ZX, (X, "Z"): MX, (X, "M"): ZX,
        }
        return source if way == "C" and source != OWN else fixed[source, way]

    def guard(ok, action):
        if ok is None:
            action()
        else:
            pl.when(ok)(action)

    def masked(slot, value, other):
        ok = valid(names[slot])
        return value if ok is None else jnp.where(ok, value, other)

    def across(slot, value):
        return masked(slot, value, 0.0) if slot in (X, MX, ZX) else value

    def inner_rows(action):
        pl.when(inner)(action)

    loads = [
        pltpu.make_async_copy(source, target, in_sem.at[index])
        for index, (source, target) in enumerate(
            ((k_in, codes.at[0]), (v_in, codes.at[1]), (q_in, data.at[OWN, QUERY]), (g_in, data.at[OWN, GRAD]))
        )
    ]
    for load in loads:
        load.start()

    barrier = pltpu.get_barrier_semaphore()
    count = jnp.int32(1)
    for slot in range(1, SLOTS):
        ok = valid(names[slot])
        if ok is not None:
            count = count + ok.astype(jnp.int32)

        def greet():
            pl.semaphore_signal(barrier, inc=1, device_id=device(names[slot]), device_id_type=MESH)

        guard(ok, greet)

    for acc in (dq_acc, dk_acc, dv_acc):
        acc[...] = jnp.zeros_like(acc)

    for name, slots in (("M", (AM, BM)), ("Z", (AZ, BZ))):
        @pl.when(jnp.logical_not(has[name]))
        def _():
            for slot in slots:
                data[slot] = jnp.zeros_like(data[slot])
                stats[slot] = jnp.zeros_like(stats[slot])

    @pl.when(outer)
    def _():
        for slot in (X, MX, ZX):
            m_rec[slot] = jnp.full_like(m_rec[slot], -1e30)
            l_rec[slot] = jnp.zeros_like(l_rec[slot])
            w_rec[slot] = jnp.zeros_like(w_rec[slot])

    blocks = k_scales.shape[0]
    block = tokens // blocks

    def scale_codes(index, part, scales):
        loads[index].wait()
        for place in range(blocks):
            span = pl.ds(place * block, block)
            scale = scales[slot_in[0, place]]
            data[OWN, part, span, :] = (codes[index, span, :].astype(jnp.float32) * scale).astype(jnp.bfloat16)

    sent = []

    def send(part, source, way):
        target = lands(source, way)
        index = len([other for other in sent[:sent.index((part, source, way))] if other[0] == part])
        return pltpu.make_async_remote_copy(
            src_ref=data.at[source, part],
            dst_ref=data.at[target, part],
            send_sem=send_sem.at[part, index],
            recv_sem=recv_sem.at[part, target],
            device_id=device(way),
            device_id_type=MESH,
        )

    def condition(source, way):
        ok = valid(names[source] + way)
        if way == "C" and source in (AM, AZ):
            ok = inner if ok is None else ok & inner
        if way == "C" and source in (BM, BZ):
            ok = outer if ok is None else ok & outer
        return ok

    def push(part, source, way, only=None):
        if (part, source, way) not in sent:
            sent.append((part, source, way))
        ok = condition(source, way)
        if only is not None:
            ok = only if ok is None else ok & only
        guard(ok, lambda: send(part, source, way).start())

    def arrive(part, slot):
        copy = pltpu.make_async_remote_copy(
            src_ref=data.at[slot, part],
            dst_ref=data.at[slot, part],
            send_sem=send_sem.at[part, 0],
            recv_sem=recv_sem.at[part, slot],
            device_id=device(names[slot]),
            device_id_type=MESH,
        )
        guard(valid(names[slot]), copy.wait_recv)

    def relay(part, slot):
        arrive(part, slot)
        if slot in (AM, AZ, BM, BZ):
            push(part, slot, "C")
        if slot in (AM, AZ) and part in (KEY, QUERY):
            push(part, slot, "X")
        if slot == X and part in (VALUE, GRAD):
            push(part, slot, "M")
            push(part, slot, "Z")

    starts, total = [], 0
    for tile in range(tiles):
        first, last = near_range(tile, tiles)
        starts.append(total)
        total += last - first

    def columns(tile):
        first, last = near_range(tile, tiles)
        return first, last, pl.ds(tile * TILE_TOKENS, TILE_TOKENS), pl.ds(starts[tile], last - first)

    units = [
        (tile, start, pl.ds(starts[tile] + start - near_range(tile, tiles)[0], TILE_TOKENS))
        for tile in range(tiles)
        for start in range(*near_range(tile, tiles), TILE_TOKENS)
    ]

    def mix(*strands):
        marks = sorted(
            ((place + 0.5) / len(steps), which, place)
            for which, steps in enumerate(strands)
            for place in range(len(steps))
        )
        for _, which, place in marks:
            strands[which][place]()

    def op_s(slot):
        held = {}

        def unit(tile, start, place):
            own = pl.ds(tile * TILE_TOKENS, TILE_TOKENS)
            scores = dot_nt(data[slot, KEY, start:start + TILE_TOKENS, :], data[OWN, QUERY, own, :]) * LOG2_SCALE
            e_all[slot, place, :] = scores
            new = jnp.max(scores, axis=0, keepdims=True)
            held[tile] = new if tile not in held else jnp.maximum(held[tile], new)
            if start + TILE_TOKENS == near_range(tile, tiles)[1]:
                m_rec[slot, :, own] = held[tile]

        return [functools.partial(unit, *item) for item in units]

    def op_d(slot):
        def unit(tile, start, place):
            own = pl.ds(tile * TILE_TOKENS, TILE_TOKENS)
            dp_all[slot, place, :] = dot_nt(data[slot, VALUE, start:start + TILE_TOKENS, :], data[OWN, GRAD, own, :])

        return [functools.partial(unit, *item) for item in units]

    def op_e(slot):
        held = {}

        def unit(tile, start, place):
            own = pl.ds(tile * TILE_TOKENS, TILE_TOKENS)
            if ("top", tile) not in held:
                held["top", tile] = m_rec[slot, :, own]
            e = jnp.exp2(e_all[slot, place, :] - held["top", tile])
            added = jnp.sum(e, axis=0, keepdims=True)
            held[tile] = added if tile not in held else held[tile] + added
            e_all[slot, place, :] = e
            if start + TILE_TOKENS == near_range(tile, tiles)[1]:
                m_rec[slot, :, own] = masked(slot, held["top", tile], -1e30)
                l_rec[slot, :, own] = masked(slot, held[tile], 0.0)

        return [functools.partial(unit, *item) for item in units]

    def op_w(slot):
        held = {}

        def unit(tile, start, place):
            added = jnp.sum(e_all[slot, place, :] * dp_all[slot, place, :], axis=0, keepdims=True)
            held[tile] = added if tile not in held else held[tile] + added
            if start + TILE_TOKENS == near_range(tile, tiles)[1]:
                w_rec[slot, :, pl.ds(tile * TILE_TOKENS, TILE_TOKENS)] = masked(slot, held[tile], 0.0)

        return [functools.partial(unit, *item) for item in units]

    def stats_send(slot):
        back = {C: C, X: X, MX: ZX, ZX: MX}.get(slot)
        if slot in (AM, BM):
            back = jnp.where(inner, AZ, BZ)
        if slot in (AZ, BZ):
            back = jnp.where(inner, AM, BM)
        return pltpu.make_async_remote_copy(
            src_ref=stats.at[OWN],
            dst_ref=stats.at[back],
            send_sem=st_send.at[slot],
            recv_sem=st_recv.at[back],
            device_id=device(names[slot]),
            device_id_type=MESH,
        )

    def op_total():
        top = m_rec[OWN]
        for slot in range(1, SLOTS):
            top = jnp.maximum(top, m_rec[slot])
        total = l_rec[OWN] * jnp.exp2(m_rec[OWN] - top)
        weighed = w_rec[OWN] * jnp.exp2(m_rec[OWN] - top)
        for slot in range(1, SLOTS):
            factor = jnp.exp2(m_rec[slot] - top)
            total += l_rec[slot] * factor
            weighed += w_rec[slot] * factor
        stats[OWN, 0:1, :] = top + jnp.log2(total)
        stats[OWN, 1:2, :] = weighed / total

    def op_q(slot, to):
        held = {}

        def unit(tile, start, place):
            own = pl.ds(tile * TILE_TOKENS, TILE_TOKENS)
            rows_of = pl.ds(start, TILE_TOKENS)
            if tile not in held:
                held[tile] = jnp.exp2(m_rec[slot, :, own] - stats[OWN, 0:1, own])
            if ("turned", start) not in held:
                held["turned", start] = data[slot, KEY, rows_of, :].T
            prob = e_all[slot, place, :] * held[tile]
            dscore = (prob * (dp_all[slot, place, :] - stats[OWN, 1:2, own])).astype(jnp.bfloat16)
            if to is not None:
                ps[to, rows_of, own] = prob.astype(jnp.bfloat16)
                ds[to, rows_of, own] = dscore
            added = jnp.dot(held["turned", start], dscore, preferred_element_type=jnp.float32)
            held["sum", tile] = added if ("sum", tile) not in held else held["sum", tile] + added
            if start + TILE_TOKENS == near_range(tile, tiles)[1]:
                dq_acc[:, own] += across(slot, held["sum", tile])

        return [functools.partial(unit, *item) for item in units]

    def op_ks(slot):
        def unit(index, tile, start, place):
            own, near = pl.ds(tile * TILE_TOKENS, TILE_TOKENS), pl.ds(start, TILE_TOKENS)
            held = pl.ds(index * TILE_TOKENS, TILE_TOKENS)
            scores = dot_nt(data[OWN, KEY, own, :], data[slot, QUERY, near, :])
            e_all[slot, held, :] = scores * LOG2_SCALE

        return [functools.partial(unit, index, *item) for index, item in enumerate(units)]

    def op_kd(slot):
        def unit(index, tile, start, place):
            own, near = pl.ds(tile * TILE_TOKENS, TILE_TOKENS), pl.ds(start, TILE_TOKENS)
            held = pl.ds(index * TILE_TOKENS, TILE_TOKENS)
            dp_all[slot, held, :] = dot_nt(data[OWN, VALUE, own, :], data[slot, GRAD, near, :])

        return [functools.partial(unit, index, *item) for index, item in enumerate(units)]

    def op_kv(slot, to):
        def unit(index, tile, start, place):
            own, near = pl.ds(tile * TILE_TOKENS, TILE_TOKENS), pl.ds(start, TILE_TOKENS)
            held = pl.ds(index * TILE_TOKENS, TILE_TOKENS)
            prob = jnp.exp2(e_all[slot, held, :] - stats[slot, 0:1, near])
            ps[to, own, near] = prob.astype(jnp.bfloat16)
            ds[to, own, near] = (prob * (dp_all[slot, held, :] - stats[slot, 1:2, near])).astype(jnp.bfloat16)

        return [functools.partial(unit, index, *item) for index, item in enumerate(units)]

    def op_m(slot, source):
        queries_of = OWN if slot == C else slot
        held = {}

        def unit(which, tile):
            part, right, acc = ((QUERY, ds, dk_acc), (GRAD, ps, dv_acc))[which]
            first, last, own, place = columns(tile)
            if which not in held:
                held[which] = data[queries_of, part].T
            summed = dot_nt(held[which][:, first:last], right[source, own, first:last])
            if part == QUERY:
                summed = summed * INVERSE
            rounded = summed.astype(jnp.bfloat16)
            if slot == C:
                part_out[which, :, own] = rounded
            else:
                acc[:, own] += across(slot, rounded.astype(jnp.float32))

        return [functools.partial(unit, which, tile) for tile in range(tiles) for which in range(2)]

    def parts_send():
        return pltpu.make_async_remote_copy(
            src_ref=part_out, dst_ref=part_in, send_sem=pt_send, recv_sem=pt_recv,
            device_id=device("C"), device_id_type=MESH,
        )

    def stats_arrive(slot):
        copy = pltpu.make_async_remote_copy(
            src_ref=stats.at[slot], dst_ref=stats.at[slot], send_sem=st_send.at[slot], recv_sem=st_recv.at[slot],
            device_id=device(names[slot]), device_id_type=MESH,
        )
        guard(valid(names[slot]), copy.wait_recv)

    scale_codes(0, KEY, k_scales)
    pl.semaphore_wait(barrier, count)
    push(KEY, OWN, "X")
    push(KEY, OWN, "M", inner)
    push(KEY, OWN, "Z", inner)
    push(KEY, OWN, "C")
    scale_codes(1, VALUE, v_scales)
    push(VALUE, OWN, "X")
    push(VALUE, OWN, "C")
    arrive(KEY, X)
    loads[2].wait()
    arrive(KEY, C)
    mix(op_s(X), op_s(C))

    push(KEY, OWN, "M", outer)
    push(KEY, OWN, "Z", outer)
    push(VALUE, OWN, "M", outer)
    push(VALUE, OWN, "Z", outer)
    relay(KEY, AZ)
    mix(op_s(OWN))

    relay(KEY, AM)
    push(VALUE, OWN, "M", inner)
    push(VALUE, OWN, "Z", inner)
    relay(VALUE, X)
    loads[3].wait()
    inner_rows(lambda: mix(op_e(X), op_d(X)))

    push(QUERY, OWN, "M", inner)
    push(QUERY, OWN, "Z", inner)
    mix(op_e(C), op_s(AM))

    relay(KEY, BM)
    push(GRAD, OWN, "M", inner)
    push(GRAD, OWN, "Z", inner)
    arrive(VALUE, C)
    mix(op_e(AM), op_d(C), op_s(BM), op_s(AZ))

    push(GRAD, OWN, "X")
    relay(KEY, BZ)
    mix(op_e(BM), op_e(AZ), op_d(OWN), op_s(BZ))

    relay(VALUE, BM)
    push(QUERY, OWN, "X")
    arrive(KEY, ZX)
    mix(op_e(BZ), op_d(BM), op_s(ZX))

    relay(VALUE, BZ)
    relay(VALUE, AZ)
    relay(VALUE, AM)
    arrive(KEY, MX)
    mix(op_e(OWN), op_d(AZ), op_s(MX), op_d(BZ))

    mix(op_e(MX), op_w(OWN))

    arrive(VALUE, ZX)
    mix(op_e(ZX), op_w(X), op_d(ZX), op_d(AM))

    relay(GRAD, X)
    arrive(VALUE, MX)
    mix(op_w(BM), op_w(BZ), op_w(ZX), op_d(MX))

    push(QUERY, OWN, "M", outer)
    push(QUERY, OWN, "Z", outer)
    push(GRAD, OWN, "M", outer)
    push(GRAD, OWN, "Z", outer)
    relay(QUERY, AM)
    mix(op_w(C), op_w(AZ), op_w(AM), op_w(MX))

    op_total()
    for slot in range(1, SLOTS):
        if slot != C:
            guard(valid(names[slot]), stats_send(slot).start)
    relay(QUERY, AZ)
    mix(op_q(OWN, 0), op_q(AM, None), op_q(AZ, None))

    relay(GRAD, AM)
    mix(op_q(X, None), op_q(C, 1), op_kd(AM), op_ks(AM))

    relay(GRAD, AZ)
    inner_rows(lambda: mix(op_q(ZX, None), op_q(MX, None), op_kd(X)))

    stats_arrive(AM)
    arrive(QUERY, X)
    mix(op_kv(AM, 2), op_m(OWN, 0), op_ks(X), op_m(C, 1))

    arrive(GRAD, ZX)
    mix(op_q(BZ, None), op_kd(AZ), op_kd(ZX), op_m(AM, 2))

    arrive(QUERY, MX)
    arrive(GRAD, MX)
    stats_arrive(X)
    inner_rows(lambda: mix(op_kv(X, 0), op_ks(MX), op_kd(MX)))

    stats_arrive(MX)
    arrive(QUERY, ZX)
    inner_rows(lambda: mix(op_kv(MX, 1), op_m(X, 0), op_ks(ZX)))

    relay(QUERY, BM)
    mix(op_q(BM, None), op_ks(AZ))
    dq_out[...] = (dq_acc[...] * INVERSE).astype(dq_out.dtype).T

    relay(QUERY, BZ)
    parts_send().start()
    stats_arrive(AZ)
    mix(op_kv(AZ, 0), op_ks(BZ), op_ks(BM), op_m(MX, 1))

    relay(GRAD, BZ)
    stats_arrive(ZX)
    mix(op_kv(ZX, 1), op_kd(BZ))

    relay(GRAD, BM)
    stats_arrive(BZ)
    mix(op_kv(BZ, 2), op_kd(BM), op_m(ZX, 1))

    stats_arrive(BM)
    mix(op_kv(BM, 1), op_m(BZ, 2))

    mix(op_m(BM, 1), op_m(AZ, 0))

    parts_send().wait_recv()
    dk_out[...] = (dk_acc[...] + part_in[0].astype(jnp.float32)).astype(dk_out.dtype).T
    dv_out[...] = (dv_acc[...] + part_in[1].astype(jnp.float32)).astype(dv_out.dtype).T

    for key in sent:
        guard(condition(*key[1:]), send(*key).wait_send)
    for slot in range(1, SLOTS):
        if slot != C:
            guard(valid(names[slot]), stats_send(slot).wait_send)
    parts_send().wait_send()


def put_out(dq_in, dk_in, dv_in, dq_out, dk_out, dv_out, out_sem):
    pairs = ((dq_in, dq_out), (dk_in, dk_out), (dv_in, dv_out))
    stores = [pltpu.make_async_copy(pair[0], pair[1], out_sem.at[i]) for i, pair in enumerate(pairs)]
    for store in stores:
        store.start()
    for store in stores:
        store.wait()


def per_device(queries, key_codes, value_codes, key_scales, value_scales, scale_slot, grad_out):
    rows = ROW_TILES
    frames = lax.axis_size("tm") // rows
    tokens, head_dim = queries.shape
    tiles = tokens // TILE_TOKENS
    near = sum(near_range(tile, tiles)[1] - near_range(tile, tiles)[0] for tile in range(tiles))
    shape = jax.ShapeDtypeStruct((tokens, head_dim), jnp.bfloat16)
    grads = pl.pallas_call(
        functools.partial(kernel, frames, rows),
        out_shape=(pltpu.VMEM((tokens, head_dim), jnp.bfloat16),) * 3,
        in_specs=[pl.BlockSpec(memory_space=pltpu.HBM)] * 4 + [pl.BlockSpec(memory_space=pltpu.SMEM)] * 3,
        out_specs=[pl.BlockSpec(memory_space=pltpu.VMEM)] * 3,
        scratch_shapes=[
            pltpu.VMEM((SLOTS, 4, tokens, head_dim), jnp.bfloat16),
            pltpu.VMEM((2, tokens, head_dim), jnp.bfloat16),
            pltpu.VMEM((SLOTS, 2, tokens), jnp.float32),
            pltpu.VMEM((SLOTS, near, TILE_TOKENS), jnp.float32),
            pltpu.VMEM((SLOTS, near, TILE_TOKENS), jnp.float32),
            pltpu.VMEM((3, tokens, tokens), jnp.bfloat16),
            pltpu.VMEM((3, tokens, tokens), jnp.bfloat16),
            pltpu.VMEM((SLOTS, 1, tokens), jnp.float32),
            pltpu.VMEM((SLOTS, 1, tokens), jnp.float32),
            pltpu.VMEM((SLOTS, 1, tokens), jnp.float32),
            pltpu.VMEM((head_dim, tokens), jnp.float32),
            pltpu.VMEM((head_dim, tokens), jnp.float32),
            pltpu.VMEM((head_dim, tokens), jnp.float32),
            pltpu.VMEM((2, head_dim, tokens), jnp.bfloat16),
            pltpu.VMEM((2, head_dim, tokens), jnp.bfloat16),
            pltpu.SemaphoreType.DMA((4,)),
            pltpu.SemaphoreType.DMA((4, 10)),
            pltpu.SemaphoreType.DMA((4, SLOTS)),
            pltpu.SemaphoreType.DMA((SLOTS,)),
            pltpu.SemaphoreType.DMA((SLOTS,)),
            pltpu.SemaphoreType.DMA,
            pltpu.SemaphoreType.DMA,
        ],
        compiler_params=pltpu.CompilerParams(
            collective_id=0, has_side_effects=True, vmem_limit_bytes=60 * 1024 * 1024
        ),
    )(queries, key_codes, value_codes, grad_out, key_scales, value_scales, scale_slot)
    return tuple(pl.pallas_call(
        put_out,
        out_shape=(shape, shape, shape),
        in_specs=[pl.BlockSpec(memory_space=pltpu.VMEM)] * 3,
        out_specs=[pl.BlockSpec(memory_space=pl.ANY)] * 3,
        scratch_shapes=[pltpu.SemaphoreType.DMA((3,))],
        compiler_params=pltpu.CompilerParams(vmem_limit_bytes=2 * 1024 * 1024),
    )(*grads))


def solution(mesh):
    in_specs = (
        P(("grp", "tm"), None),
        P(("grp", "tm"), None),
        P(("grp", "tm"), None),
        P(("grp", "tm")),
        P(("grp", "tm")),
        P(("grp", "tm"), None),
        P(("grp", "tm"), None),
    )
    out_specs = (P(("grp", "tm"), None), P(("grp", "tm"), None), P(("grp", "tm"), None))
    return jax.shard_map(
        per_device, mesh=mesh, in_specs=in_specs, out_specs=out_specs, check_vma=False
    )
```
